128 devices in a mesh: seq: 4 (over z_lo, core), vocab: 32 (over y, x, z_hi).
Axes of the slice: x: 4, y: 4, z: 4 (z_hi: 2, z_lo: 2; z = z_hi * 2 + z_lo), core: 2. Of those that a mesh axis runs over, the one named last changes fastest.
Arguments:
- hidden: bfloat16 [512, 8192], P('seq'), may hold values from -6 to 6
- steer: float32 [8192], replicated, may hold values from -4 to 4
- tangent: float32 [8192], replicated, may hold values from -6 to 6
- gain: float32 [8192], replicated, may hold values from 0.5 to 1.5
- head: bfloat16 [8192, 77824], P('seq', 'vocab'), may hold values from -0.198873782 to 0.198873782
- target: bfloat16 [512, 77824], P('seq', 'vocab'), may hold values from 0.099609375 to 10
Outputs:
- gradient: float32 [512, 8192], P('vocab', 'seq')
- curvature: float32 [512, 8192], P('vocab', 'seq')
The draws below stay inside these ranges and needn't reach their ends.
All inputs are finite; a program needn't handle non-finite values.
Results may differ from the reference program's by a relative error of at most 0.0082.
Values may be sent and summed in bfloat16 or wider, within the bound.
A program may use at most 128 MiB of HBM per device.

```python
import math
import jax
import jax.numpy as jnp
from jax import lax

D = 8192
VOCAB = 77824
TOKENS = 512


def draw_hidden(key, part):
    values = jnp.clip(jax.random.normal(key, (TOKENS, D), jnp.float32), -6.0, 6.0)
    return values.astype(jnp.bfloat16)


def draw_head(key, part):
    spread = 3.0 / math.sqrt(D)
    values = jnp.clip(jax.random.normal(jax.random.fold_in(key, 5), (D, VOCAB), jnp.float32), -6.0, 6.0) * spread
    return values.astype(jnp.bfloat16)


def steps_of(stream_key, extent, split, least, high):
    factor_of, own = 1.0, jax.random.fold_in(stream_key, 6)
    for position, blocks in split:
        draws = jnp.exp(jax.random.uniform(jax.random.fold_in(own, position), (blocks,), jnp.float32, least / len(split), high / len(split)))
        factor_of = factor_of * jnp.repeat(draws, extent[position] // blocks).reshape([-1 if axis == position else 1 for axis in range(len(extent))])
    return factor_of


def gaussian(stream_key, shape, deviation, bound, kind=jnp.bfloat16):
    return jnp.clip(deviation * jax.random.normal(stream_key, shape, jnp.float32), -bound, bound).astype(kind)


def setup_inputs(seed: int = 0) -> dict:
    splits = jax.random.split(jax.random.key(seed), 7)
    return {
        "hidden": draw_hidden(jax.random.fold_in(splits[6], 71), 0),
        "steer": gaussian(splits[1], (D,), 0.3, 4.0, jnp.float32),
        "tangent": gaussian(splits[2], (D,), 1.0, 6.0, jnp.float32),
        "gain": jnp.clip(1.0 + 0.1 * jax.random.normal(splits[3], (D,), jnp.float32), 0.5, 1.5),
        "head": draw_head(jax.random.fold_in(splits[6], 71), 0),
        "target": jnp.clip(jnp.exp(math.log(10.0) - 4.609084 * jax.random.uniform(splits[5], (TOKENS, VOCAB), jnp.float32) ** steps_of(splits[5], (TOKENS, VOCAB), ((0, 4), (1, 32)), -0.2, 0.2)), 0.099609375, 10.0).astype(jnp.bfloat16),
    }


EPSILON = 1e-06

def reference(hidden, steer, tangent, gain, head, target):
    inputs = hidden.astype(jnp.float32) + steer
    feature_count = inputs.shape[1]
    meansq = lax.optimization_barrier(jnp.sum(inputs * inputs, axis=1)) / feature_count
    denominator = meansq + EPSILON
    radius = jnp.sqrt(denominator)
    tangent_dot = lax.optimization_barrier(jnp.sum(inputs * tangent, axis=1)) / feature_count
    normed = (gain * inputs / radius[:, None]).astype(jnp.bfloat16)
    tangent_normed = (gain * (tangent - inputs * (tangent_dot / denominator)[:, None]) / radius[:, None]).astype(jnp.bfloat16)
    logits = jnp.dot(normed, head, preferred_element_type=jnp.float32)
    dlogits = jnp.dot(tangent_normed, head, preferred_element_type=jnp.float32)
    row_peak = lax.optimization_barrier(jnp.max(logits, axis=1, keepdims=True))
    exponent = jnp.exp(logits - row_peak)
    row_total = lax.optimization_barrier(jnp.sum(exponent, axis=1))
    softmax_probs = exponent / row_total[:, None]
    mean_shift = lax.optimization_barrier(jnp.sum(exponent * dlogits, axis=1)) / row_total
    weights = target.astype(jnp.float32)
    target_probs = weights / lax.optimization_barrier(jnp.sum(weights, axis=1))[:, None]
    cot_grad = (softmax_probs - target_probs).astype(jnp.bfloat16)
    cot_ggn = (softmax_probs * (dlogits - mean_shift[:, None])).astype(jnp.bfloat16)
    dims = (((1,), (1,)), ((), ()))
    back_grad = lax.dot_general(cot_grad, head, dims, preferred_element_type=jnp.float32)
    back_ggn = lax.dot_general(cot_ggn, head, dims, preferred_element_type=jnp.float32)

    def norm_back(upstream):
        scaled = gain * upstream
        dotted = lax.optimization_barrier(jnp.sum(inputs * scaled, axis=1)) / feature_count
        return (scaled - inputs * (dotted / denominator)[:, None]) / radius[:, None]
    return (norm_back(back_grad), norm_back(back_ggn))
```

```python
import jax
import jax.numpy as jnp
from jax import lax
from jax.experimental import pallas as pl
from jax.experimental.pallas import tpu as pltpu
from jax.sharding import PartitionSpec as P

EPSILON = 1e-06
MESH = pl.DeviceIdType.MESH
F32 = jnp.float32
BF16 = jnp.bfloat16
NT = (((1,), (1,)), ((), ()))
ROWS = 16
KNEE = 8.0
POWER = 32
SHIFT = 126.0 / POWER


def encode(value):
    code = (1.0 + jnp.abs(value) * (1.0 / KNEE)) * (2.0**-SHIFT)
    for _ in range(5):
        code = code * code
    return jnp.where(value < 0, -code, code).astype(BF16)


def decode(code):
    code = code.astype(F32)
    root = jnp.exp2(jnp.log2(jnp.abs(code)) * (1.0 / POWER) + SHIFT)
    size = (root - 1.0) * KNEE
    return jnp.where(code < 0, -size, size)


def lanes(columns):
    rows = columns[0].shape[0]
    lane = lax.broadcasted_iota(jnp.int32, (rows, 128), 1)
    out = jnp.zeros((rows, 128), F32)
    for place, column in enumerate(columns):
        out = jnp.where(lane == place, column, out)
    return out


def kernel(
    hidden, head_hbm, target, steer, tangent, gain,
    out_grad, out_ggn,
    hfull, hid, stats_in, sq, head, nrm_loc, nrm_rem, upart, uvec, part, psib, code_out, code_in, tgt,
    e_ref, f_ref, gt, ge, gf, norm_col, st_col, st_row, st_in, fin_row, fin_col,
    sb, ropp, rraw, racc, s2, r2, t2, s3, r3,
    loc_sem, hs_s, hs_r, ss_s, ss_r, us_s, us_r, ts_s, ts_r, tf_s, tf_r, ps_s, ps_r, cs_s, cs_r, cf_s, cf_r,
    xs_s, xs_r, a_s, a_r, b_s, b_r, z_s, z_r,
):
    s = lax.axis_index("seq")
    v = lax.axis_index("vocab")
    zl, c = s // 2, s % 2
    y, x, zh = v // 8, (v // 2) % 4, v % 2
    depth = 2048
    width = 2432
    full = 8192
    sib = {"seq": 2 * zl + 1 - c, "vocab": v}
    flip = {"seq": s, "vocab": v + 1 - 2 * zh}

    def pair(core):
        return {"seq": 2 * (1 - zl) + core, "vocab": v}

    def zo(core):
        return {"seq": 2 * (1 - zl) + core, "vocab": v + 1 - 2 * zh}

    def xn(k):
        return {"seq": s, "vocab": y * 8 + ((x + k) % 4) * 2 + zh}

    def yn(k):
        return {"seq": s, "vocab": ((y + k) % 4) * 8 + x * 2 + zh}

    def rc(src, dst, ssem, rsem, dev):
        return pltpu.make_async_remote_copy(
            src_ref=src, dst_ref=dst, send_sem=ssem, recv_sem=rsem, device_id=dev, device_id_type=MESH
        )

    sends = []

    def go(*args):
        copy = rc(*args)
        copy.start()
        sends.append(copy)

    load_head = pltpu.make_async_copy(head_hbm, head, loc_sem.at[0])
    load_hfull = pltpu.make_async_copy(hidden, hfull, loc_sem.at[1])
    my_cols = pl.ds(pl.multiple_of(s * depth, depth), depth)
    load_tgt = pltpu.make_async_copy(target, tgt.at[c], loc_sem.at[2])
    load_own = pltpu.make_async_copy(hidden.at[:, my_cols], hid.at[c], loc_sem.at[3])
    load_hfull.start()
    load_own.start()
    load_head.start()
    load_tgt.start()

    barrier = pltpu.get_barrier_semaphore()
    peers = [sib, pair(0), pair(1), zo(0), zo(1), flip] + [xn(k) for k in (1, 2, 3)] + [yn(k) for k in (1, 2, 3)]
    for peer in peers:
        pl.semaphore_signal(barrier, inc=1, device_id=peer, device_id_type=MESH)
    pl.semaphore_wait(barrier, len(peers))

    def cols_of(seq):
        return pl.ds(pl.multiple_of(seq * depth, depth), depth)

    go(hidden.at[:, cols_of(2 * zl + 1 - c)], hid.at[c], hs_s.at[0], hs_r.at[c], sib)
    for core in range(2):
        go(hidden.at[:, cols_of(2 * (1 - zl) + core)], hid.at[2 + c], hs_s.at[1 + core], hs_r.at[2 + c], zo(core))
    go(target, tgt.at[c], ts_s.at[0], ts_r.at[c], sib)

    load_hfull.wait()

    def sums(i, carry):
        rows = pl.ds(pl.multiple_of(i * ROWS, ROWS), ROWS)
        squares = jnp.zeros((ROWS, 1), F32)
        dots = jnp.zeros((ROWS, 1), F32)
        for q in range(8):
            cols = pl.ds(q * 1024, 1024)
            inputs = hfull[rows, cols].astype(F32) + steer[:, cols]
            squares += jnp.sum(inputs * inputs, axis=1, keepdims=True)
            dots += jnp.sum(inputs * tangent[:, cols], axis=1, keepdims=True)
        sq[rows, :] = lanes([squares, dots])
        return carry

    lax.fori_loop(0, 128 // ROWS, sums, 0)
    stats_in[c] = sq[...].T[0:8, :]
    for place, dev in enumerate((sib, pair(0), pair(1))):
        slot = c if place == 0 else 2 + c
        go(stats_in.at[c], stats_in.at[slot], ss_s.at[place], ss_r.at[slot], dev)
    go(target, tgt.at[2 + c], ts_s.at[1], ts_r.at[2 + c], pair(c))

    steer_part = steer[:, my_cols]
    gain_part = gain[:, my_cols]
    other = 1 - c

    def norm_block(p, dest, base):
        sq[...] = jnp.zeros((128, 128), F32)
        sq[0:8, :] = stats_in[p]
        sq[...] = sq[...].T

        def rows_of(i, carry):
            rows = pl.ds(pl.multiple_of(i * ROWS, ROWS), ROWS)
            both = sq[rows, :]
            denominator = both[:, 0:1] / full + EPSILON
            radius = jnp.sqrt(denominator)
            inverse = 1.0 / radius
            norm_col[p, rows, :] = lanes([inverse, both[:, 1:2] / full / denominator, radius])
            inputs = hid[p, rows, :].astype(F32) + steer_part
            dest[pl.ds(pl.multiple_of(i * ROWS + base, ROWS), ROWS), :] = (gain_part * inputs * inverse).astype(BF16)
            return carry

        lax.fori_loop(0, 128 // ROWS, rows_of, 0)

    def recv(dst, ssem, rsem):
        rc(dst, dst, ssem, rsem, sib).wait_recv()

    product = gain_part * tangent[:, my_cols]
    high = product.astype(BF16).astype(F32)
    row = lax.broadcasted_iota(jnp.int32, (16, depth), 0)
    nrm_loc[256:272, :] = jnp.where(row == 0, high, jnp.where(row == 1, product - high, 0.0)).astype(BF16)

    load_own.wait()
    recv(hid.at[other], hs_s.at[0], hs_r.at[other])
    recv(stats_in.at[other], ss_s.at[0], ss_r.at[other])
    norm_block(0, nrm_loc, 0)
    norm_block(1, nrm_loc, 128)
    load_head.wait()

    tiles = [(0, 512), (512, 512), (1024, 512), (1536, 512), (2048, 384)]
    for start, size in tiles:
        got = jnp.dot(nrm_loc[...], head[:, start : start + size], preferred_element_type=F32)
        part[0, :, start : start + size] = got[0:128]
        part[1, :, start : start + size] = got[128:256]
        upart[s, :, start : start + size] = jnp.sum(got[256:272], axis=0, keepdims=True)
    for p in range(2):
        rc(part.at[p], psib.at[p], ps_s.at[p], ps_r.at[p], sib).start()
    for place, dev in enumerate((sib, pair(0), pair(1))):
        go(upart.at[s], upart.at[s], us_s.at[place], us_r.at[s], dev)

    load_tgt.wait()
    recv(tgt.at[other], ts_s.at[0], ts_r.at[other])

    def target_product(p0):
        def tile(n, carry):
            cols = pl.ds(pl.multiple_of(n * 256, 256), 256)
            lhs = tgt[p0 : p0 + 2].reshape(256, width)
            got = lax.dot_general(lhs, head[cols, :], NT, preferred_element_type=F32)
            gt[pl.ds(p0 * 128, 256), cols] = got
            return carry

        lax.fori_loop(0, 8, tile, 0)

    target_product(0)

    def chip_sum(p0):
        for p in (p0, p0 + 1):
            recv(psib.at[p], ps_s.at[p], ps_r.at[p])

            def rows_of(i, carry):
                rows = pl.ds(pl.multiple_of(i * ROWS, ROWS), ROWS)
                part[p, rows, :] = part[p, rows, :] + psib[p, rows, :]
                return carry

            rc(part.at[p], psib.at[p], ps_s.at[p], ps_r.at[p], sib).wait_send()
            lax.fori_loop(0, 128 // ROWS, rows_of, 0)
        half = p0 // 2

        def code_rows(i, carry):
            rows = pl.ds(pl.multiple_of(i * ROWS, ROWS), ROWS)
            code_out[half, rows, :] = encode(part[p0 + c, rows, :])
            return carry

        lax.fori_loop(0, 128 // ROWS, code_rows, 0)
        go(code_out.at[half], code_in.at[2 - p0 + c], cs_s.at[half], cs_r.at[2 - p0 + c], pair(c))

    chip_sum(0)

    recv(tgt.at[2 + c], ts_s.at[1], ts_r.at[2 + c])
    go(tgt.at[2 + c], tgt.at[2 + c], tf_s.at[0], tf_r.at[c], sib)
    recv(tgt.at[2 + other], tf_s.at[0], tf_r.at[other])
    target_product(2)

    for core in range(2):
        recv(hid.at[2 + core], hs_s.at[1], hs_r.at[2 + core])
        recv(stats_in.at[2 + core], ss_s.at[1], ss_r.at[2 + core])
        norm_block(2 + core, nrm_rem, 128 * core)
    for start, size in tiles:
        got = jnp.dot(nrm_rem[...], head[:, start : start + size], preferred_element_type=F32)
        part[2, :, start : start + size] = got[0:128]
        part[3, :, start : start + size] = got[128:256]
    for p in (2, 3):
        rc(part.at[p], psib.at[p], ps_s.at[p], ps_r.at[p], sib).start()
    chip_sum(2)

    recv(upart.at[2 * zl + other], us_s.at[0], us_r.at[2 * zl + other])
    for core in range(2):
        recv(upart.at[2 * (1 - zl) + core], us_s.at[1], us_r.at[2 * (1 - zl) + core])
    uvec[...] = (upart[0] + upart[1]) + (upart[2] + upart[3])

    def softmax_rows(p):
        def rows_of(i, carry):
            rows = pl.ds(pl.multiple_of(i * ROWS, ROWS), ROWS)
            logits = part[p, rows, :] + decode(code_in[p, rows, :])
            part[p, rows, :] = logits
            peak = jnp.max(logits, axis=1, keepdims=True)
            columns = norm_col[p, rows, :]
            inverse, along = columns[:, 0:1], columns[:, 1:2]
            u = uvec[...]
            exponent = jnp.exp(logits - peak)
            dlogits = u * inverse - along * logits
            total = jnp.sum(exponent, axis=1, keepdims=True)
            shift = jnp.sum(exponent * dlogits, axis=1, keepdims=True)
            first = jnp.sum(exponent * logits, axis=1, keepdims=True)
            weights = tgt[p, rows, :].astype(F32)
            weight_total = jnp.sum(weights, axis=1, keepdims=True)
            weight_first = jnp.sum(weights * logits, axis=1, keepdims=True)
            mean = shift / total
            weighted = exponent * (dlogits - mean)
            second = jnp.sum(weighted * logits, axis=1, keepdims=True) + mean * first
            e_ref[p, rows, :] = exponent.astype(BF16)
            f_ref[p, rows, :] = weighted.astype(BF16)
            st_col[rows, :] = lanes([peak, total, shift, first, second, weight_total, weight_first])
            return carry

        lax.fori_loop(0, 128 // ROWS, rows_of, 0)
        st_row[p] = st_col[...].T[0:8, :]

    for p0 in (2, 0):
        recv(code_in.at[p0 + c], cs_s.at[0], cs_r.at[p0 + c])
        go(code_in.at[p0 + c], code_in.at[p0 + c], cf_s.at[p0 // 2], cf_r.at[p0 // 2], sib)
        recv(code_in.at[p0 + other], cf_s.at[p0 // 2], cf_r.at[p0 // 2])
        softmax_rows(p0)
        softmax_rows(p0 + 1)

    def merge(a, b):
        peak = jnp.maximum(a[:, 0:1], b[:, 0:1])
        lane = lax.broadcasted_iota(jnp.int32, (4, 8, 128), 1)
        scale_a = jnp.where(lane < 5, jnp.exp(a[:, 0:1] - peak), 1.0)
        scale_b = jnp.where(lane < 5, jnp.exp(b[:, 0:1] - peak), 1.0)
        return jnp.where(lane == 0, peak, a * scale_a + b * scale_b)

    st_in[7] = st_row[...]
    for stage, hop in enumerate((xn, yn)):
        for k in (1, 2, 3):
            slot = 3 * stage + k - 1
            go(st_in.at[7 + stage], st_in.at[slot], xs_s.at[slot], xs_r.at[slot], hop(k))
        total = st_in[7 + stage]
        for k in (1, 2, 3):
            slot = 3 * stage + k - 1
            recv(st_in.at[slot], xs_s.at[slot], xs_r.at[slot])
            total = merge(total, st_in[slot])
        st_in[8 + stage] = total
    go(st_in.at[9], st_in.at[6], xs_s.at[6], xs_r.at[6], flip)
    recv(st_in.at[6], xs_s.at[6], xs_r.at[6])
    total = merge(st_in[9], st_in[6])
    for p in range(4):
        mine = st_row[p]
        sums_of = total[p]
        factor = jnp.exp(mine[0:1] - sums_of[0:1]) / sums_of[1:2]
        shift = sums_of[2:3] / sums_of[1:2]
        turn = factor * (mine[2:3] / mine[1:2] - shift)
        weight = 1.0 / sums_of[5:6]
        mean_logit = sums_of[3:4] / sums_of[1:2]
        dot_grad = mean_logit - sums_of[6:7] * weight
        dot_ggn = sums_of[4:5] / sums_of[1:2] - shift * mean_logit
        sq[...] = jnp.zeros((128, 128), F32)
        for place, line in enumerate((factor, turn, weight, dot_grad, dot_ggn)):
            sq[place : place + 1, :] = line
        fin_col[p] = sq[...].T

    def ring(o, stage):
        along_x = o == stage
        if along_x:
            return xn(1), xn(3), lambda k: (x + k) % 4
        return yn(1), yn(3), lambda k: (y + k + 2 * zl) % 4

    def stage1(o, n):
        right, left, at = ring(o, 0)
        opp = [
            rc(sb.at[o, n, 0, at(2)], ropp.at[o, n, 0], a_s.at[o, n, 0], a_r.at[o, n, 0], right),
            rc(sb.at[o, n, 1, at(2)], ropp.at[o, n, 1], a_s.at[o, n, 1], a_r.at[o, n, 1], left),
        ]
        raw = [
            rc(sb.at[o, n, 1, at(1)], rraw.at[o, n, 1], a_s.at[o, n, 2], a_r.at[o, n, 2], right),
            rc(sb.at[o, n, 0, at(3)], rraw.at[o, n, 0], a_s.at[o, n, 3], a_r.at[o, n, 3], left),
        ]
        acc = [
            rc(sb.at[o, n, 0, at(1)], racc.at[o, n, 0], a_s.at[o, n, 4], a_r.at[o, n, 4], right),
            rc(sb.at[o, n, 1, at(3)], racc.at[o, n, 1], a_s.at[o, n, 5], a_r.at[o, n, 5], left),
        ]
        return at, opp, raw, acc

    def relay(n):
        for o in range(2):
            at, opp, raw, acc = stage1(o, n)
            for h in range(2):
                opp[h].wait_recv()
                where = at(1) if h == 0 else at(3)
                sb[o, n, h, where] = (sb[o, n, h, where].astype(F32) + ropp[o, n, h].astype(F32)).astype(BF16)
                acc[h].start()

    def chunk(n, carry):
        cols = pl.ds(pl.multiple_of(n * 512, 512), 512)
        block = head[cols, :]
        ge[...] = lax.dot_general(e_ref[...].reshape(512, width), block, NT, preferred_element_type=F32)
        gf[...] = lax.dot_general(f_ref[...].reshape(512, width), block, NT, preferred_element_type=F32)
        for p in range(4):
            for k in range(4):
                rows = pl.ds(p * 128 + k * 32, 32)
                columns = fin_col[p, pl.ds(k * 32, 32), :]
                factor, turn, weight = columns[:, 0:1], columns[:, 1:2], columns[:, 2:3]
                value = ge[rows, :]
                grad = factor * value - weight * gt[rows, cols]
                ggn = factor * gf[rows, :] + turn * value
                for h in range(2):
                    sb[0, n, h, k, pl.ds(p * 32, 32), :] = grad[:, h * 256 : (h + 1) * 256].astype(BF16)
                    sb[1, n, h, p, pl.ds(k * 32, 32), :] = ggn[:, h * 256 : (h + 1) * 256].astype(BF16)
        for o in range(2):
            at, opp, raw, acc = stage1(o, n)
            for copy in opp + raw:
                copy.start()

        @pl.when(n > 0)
        def _():
            relay(n - 1)

        return carry

    lax.fori_loop(0, 4, chunk, 0)
    relay(3)

    for n in range(4):
        for o in range(2):
            at, opp, raw, acc = stage1(o, n)
            for h in range(2):
                raw[1 - h].wait_recv()
                acc[h].wait_recv()
                mine = sb[o, n, h, at(0)].astype(F32) + racc[o, n, h].astype(F32) + rraw[o, n, h].astype(F32)
                first = (n % 2) * 512 + h * 256
                for d in range(4):
                    s2[o, n // 2, d, :, first : first + 256] = mine[d * 32 : (d + 1) * 32].astype(BF16)

    steps = []
    for o in range(2):
        right, left, at = ring(o, 1)
        opp = [
            rc(s2.at[o, 0, at(2)], r2.at[o, 0], b_s.at[o, 0], b_r.at[o, 0], right),
            rc(s2.at[o, 1, at(2)], r2.at[o, 1], b_s.at[o, 1], b_r.at[o, 1], left),
        ]
        raw = [
            rc(s2.at[o, 0, at(3)], r2.at[o, 2], b_s.at[o, 2], b_r.at[o, 2], left),
            rc(s2.at[o, 1, at(1)], r2.at[o, 3], b_s.at[o, 3], b_r.at[o, 3], right),
        ]
        acc = [
            rc(s2.at[o, 0, at(1)], r2.at[o, 4], b_s.at[o, 4], b_r.at[o, 4], right),
            rc(s2.at[o, 1, at(3)], r2.at[o, 5], b_s.at[o, 5], b_r.at[o, 5], left),
        ]
        for copy in opp + raw:
            copy.start()
        steps.append((at, opp, raw, acc))
    for o in range(2):
        at, opp, raw, acc = steps[o]
        for h in range(2):
            opp[h].wait_recv()
            where = at(1) if h == 0 else at(3)
            s2[o, h, where] = (s2[o, h, where].astype(F32) + r2[o, h].astype(F32)).astype(BF16)
            acc[h].start()
    last = []
    for o in range(2):
        at, opp, raw, acc = steps[o]
        for h in range(2):
            raw[h].wait_recv()
            acc[h].wait_recv()
            mine = s2[o, h, at(0)].astype(F32) + r2[o, 2 + h].astype(F32) + r2[o, 4 + h].astype(F32)
            for z in range(2):
                t2[o, z, :, h * 1024 : (h + 1) * 1024] = mine[z * 16 : (z + 1) * 16]
        s3[o] = t2[o, 1 - zh].astype(BF16)
        copy = rc(s3.at[o], r3.at[o], z_s.at[o], z_r.at[o], flip)
        copy.start()
        last.append(copy)

    p_mine = (y + 2 * zl) % 4
    rows = pl.ds(pl.multiple_of(x * 32 + zh * 16, 16), 16)
    inputs = hid[p_mine, rows, :].astype(F32) + steer_part
    inverse = norm_col[p_mine, rows, :][:, 0:1]
    columns = fin_col[p_mine, rows, :]
    for o, out in enumerate((out_grad, out_ggn)):
        last[o].wait_recv()
        back = t2[o, zh] + r3[o].astype(F32)
        slope = columns[:, 3 + o : 4 + o] * inverse * (1.0 / full)
        out[...] = (gain_part * back - inputs * slope) * inverse

    for n in range(4):
        for o in range(2):
            at, opp, raw, acc = stage1(o, n)
            for copy in opp + raw + acc:
                copy.wait_send()
    for at, opp, raw, acc in steps:
        for copy in opp + raw + acc:
            copy.wait_send()
    for copy in last:
        copy.wait_send()
    for copy in sends:
        copy.wait_send()


def body(hidden, steer, tangent, gain, head, target):
    vmem = pltpu.VMEM
    dma = pltpu.SemaphoreType.DMA
    any_spec = pl.BlockSpec(memory_space=pl.ANY)
    vmem_spec = pl.BlockSpec(memory_space=pltpu.VMEM)
    return pl.pallas_call(
        kernel,
        out_shape=[jax.ShapeDtypeStruct((16, 2048), F32)] * 2,
        in_specs=[any_spec] * 3 + [vmem_spec] * 3,
        out_specs=[vmem_spec] * 2,
        scratch_shapes=[
            vmem((128, 8192), BF16),
            vmem((4, 128, 2048), BF16),
            vmem((4, 8, 128), F32),
            vmem((128, 128), F32),
            vmem((2048, 2432), BF16),
            vmem((272, 2048), BF16),
            vmem((256, 2048), BF16),
            vmem((4, 1, 2432), F32),
            vmem((1, 2432), F32),
            vmem((4, 128, 2432), F32),
            vmem((4, 128, 2432), F32),
            vmem((2, 128, 2432), BF16),
            vmem((4, 128, 2432), BF16),
            vmem((4, 128, 2432), BF16),
            vmem((4, 128, 2432), BF16),
            vmem((4, 128, 2432), BF16),
            vmem((512, 2048), F32),
            vmem((512, 512), F32),
            vmem((512, 512), F32),
            vmem((4, 128, 128), F32),
            vmem((128, 128), F32),
            vmem((4, 8, 128), F32),
            vmem((10, 4, 8, 128), F32),
            vmem((8, 128), F32),
            vmem((4, 128, 128), F32),
            vmem((2, 4, 2, 4, 128, 256), BF16),
            vmem((2, 4, 2, 128, 256), BF16),
            vmem((2, 4, 2, 128, 256), BF16),
            vmem((2, 4, 2, 128, 256), BF16),
            vmem((2, 2, 4, 32, 1024), BF16),
            vmem((2, 6, 32, 1024), BF16),
            vmem((2, 2, 16, 2048), F32),
            vmem((2, 16, 2048), BF16),
            vmem((2, 16, 2048), BF16),
            dma((4,)),
            dma((3,)), dma((4,)),
            dma((3,)), dma((4,)),
            dma((3,)), dma((4,)),
            dma((2,)), dma((4,)),
            dma((1,)), dma((2,)),
            dma((4,)), dma((4,)),
            dma((2,)), dma((4,)),
            dma((2,)), dma((2,)),
            dma((7,)), dma((7,)),
            dma((2, 4, 6)), dma((2, 4, 6)),
            dma((2, 6)), dma((2, 6)),
            dma((2,)), dma((2,)),
        ],
        compiler_params=pltpu.CompilerParams(
            collective_id=0, has_side_effects=True, vmem_limit_bytes=66 * 1024 * 1024 - 2 * 1024 * 1024
        ),
    )(hidden, head, target, steer.reshape(1, -1), tangent.reshape(1, -1), gain.reshape(1, -1))


def solution(mesh):
    return jax.shard_map(
        body,
        mesh=mesh,
        in_specs=(P("seq", None), P(), P(), P(), P("seq", "vocab"), P("seq", "vocab")),
        out_specs=(P("vocab", "seq"), P("vocab", "seq")),
        check_vma=False,
    )
```

```python
import jax
import jax.numpy as jnp
from jax import lax
from jax.experimental import pallas as pl
from jax.experimental.pallas import tpu as pltpu
from jax.sharding import PartitionSpec as P

EPSILON = 1e-06
MESH = pl.DeviceIdType.MESH
F32 = jnp.float32
BF16 = jnp.bfloat16
NT = (((1,), (1,)), ((), ()))
ROWS = 16
KNEE = 8.0
POWER = 32
SHIFT = 126.0 / POWER


def encode(value):
    code = (1.0 + jnp.abs(value) * (1.0 / KNEE)) * (2.0**-SHIFT)
    for _ in range(5):
        code = code * code
    return jnp.where(value < 0, -code, code).astype(BF16)


def decode(code):
    code = code.astype(F32)
    root = jnp.exp2(jnp.log2(jnp.abs(code)) * (1.0 / POWER) + SHIFT)
    size = (root - 1.0) * KNEE
    return jnp.where(code < 0, -size, size)


def lanes(columns):
    rows = columns[0].shape[0]
    lane = lax.broadcasted_iota(jnp.int32, (rows, 128), 1)
    out = jnp.zeros((rows, 128), F32)
    for place, column in enumerate(columns):
        out = jnp.where(lane == place, column, out)
    return out


class Reduce:
    def __init__(self, ring, buffer, landing, send_sem, recv_sem):
        self.ring, self.buffer, self.landing = ring, buffer, landing
        self.send_sem, self.recv_sem = send_sem, recv_sem

    def copies(self, route, n):
        right, left, at = self.ring(route)

        def copy(h, kind, dest, device):
            return pltpu.make_async_remote_copy(
                src_ref=self.buffer.at[route, n, h, dest],
                dst_ref=self.landing.at[route, n, h, kind],
                send_sem=self.send_sem.at[0],
                recv_sem=self.recv_sem.at[n, min(kind, 1)],
                device_id=device,
                device_id_type=MESH,
            )

        opposite = [copy(0, 0, at(2), right), copy(1, 0, at(2), left)]
        raw = [copy(0, 1, at(3), left), copy(1, 1, at(1), right)]
        summed = [copy(0, 2, at(1), right), copy(1, 2, at(3), left)]
        return at, opposite, raw, summed

    def send(self, n):
        for route in range(2):
            _, opposite, raw, _ = self.copies(route, n)
            for copy in opposite + raw:
                copy.start()

    def all_of(self, ref, recv_sem):
        return pltpu.make_async_remote_copy(
            src_ref=ref, dst_ref=ref, send_sem=self.send_sem.at[0], recv_sem=recv_sem,
            device_id=self.ring(0)[0], device_id_type=MESH,
        )

    def relay(self, n):
        self.all_of(self.landing.at[:, n, :, 0], self.recv_sem.at[n, 0]).wait_recv()
        for route in range(2):
            at, _, _, summed = self.copies(route, n)
            for h in range(2):
                where = at(1) if h == 0 else at(3)
                mine = self.buffer[route, n, h, where].astype(F32)
                self.buffer[route, n, h, where] = (mine + self.landing[route, n, h, 0].astype(F32)).astype(BF16)
                summed[h].start()

    def wait(self, n):
        self.all_of(self.landing.at[:, n, :, 1:3], self.recv_sem.at[n, 1]).wait_recv()

    def total(self, route, n, h, o, rows):
        at = self.ring(route)[2]
        out = self.buffer[route, n, h, at(0), o, rows, :].astype(F32)
        return out + self.landing[route, n, h, 1, o, rows, :].astype(F32) + self.landing[route, n, h, 2, o, rows, :].astype(F32)

    def drain(self):
        self.all_of(self.landing, self.recv_sem.at[0, 0]).wait_send()


def kernel(
    hidden, head_hbm, target, steer, tangent, gain,
    out, out_col,
    hfull, hid, stats_in, sq, head, nrm_loc, nrm_rem, upart, uvec, part, psib, code_out, code_in, tgt,
    ef, norm_col, st_col, st_in, fin_col, wide, fin2, fin3,
    sb, r1, s2, r2, t2, s3, r3, gsb, gr1, gs2, gr2, gt2, gs3, gr3,
    loc_sem, hs_s, hs_r, fs_s, fs_r, hr_s, hr_r, ss_s, ss_r, us_s, us_r, ts_s, ts_r, tf_s, tf_r, ps_s, ps_r,
    cs_s, cs_r, cf_s, cf_r, xs_s, xs_r, a_s, a_r, b_s, b_r, z_s, z_r, ga_s, ga_r, gb_s, gb_r, gz_s, gz_r,
):
    s = lax.axis_index("seq")
    v = lax.axis_index("vocab")
    zl, c = s // 2, s % 2
    y, x, zh = v // 8, (v // 2) % 4, v % 2
    depth = 2048
    width = 2432
    full = 8192
    other = 1 - c
    p_mine = (y + 2 * zl) % 4
    sib = {"seq": 2 * zl + 1 - c, "vocab": v}
    flip = {"seq": s, "vocab": v + 1 - 2 * zh}

    def pair(core):
        return {"seq": 2 * (1 - zl) + core, "vocab": v}

    def zo(core):
        return {"seq": 2 * (1 - zl) + core, "vocab": v + 1 - 2 * zh}

    def xn(k):
        return {"seq": s, "vocab": y * 8 + ((x + k) % 4) * 2 + zh}

    def yn(k):
        return {"seq": s, "vocab": ((y + k) % 4) * 8 + x * 2 + zh}

    def ring_of(stage):
        def ring(route):
            if route == stage:
                return xn(1), xn(3), lambda k: (x + k) % 4
            return yn(1), yn(3), lambda k: (y + k + 2 * zl) % 4

        return ring

    def rc(src, dst, ssem, rsem, dev):
        return pltpu.make_async_remote_copy(
            src_ref=src, dst_ref=dst, send_sem=ssem, recv_sem=rsem, device_id=dev, device_id_type=MESH
        )

    sends = []

    def go(*args):
        copy = rc(*args)
        copy.start()
        sends.append(copy)

    def recv(dst, ssem, rsem):
        rc(dst, dst, ssem, rsem, sib).wait_recv()

    def cols_of(seq):
        return pl.ds(pl.multiple_of(seq * depth, depth), depth)

    def sixteen(i):
        return pl.ds(pl.multiple_of(i * ROWS, ROWS), ROWS)

    my_cols = cols_of(s)
    load_head = pltpu.make_async_copy(head_hbm, head, loc_sem.at[0])
    load_hfull = pltpu.make_async_copy(hidden, hfull, loc_sem.at[1])
    load_tgt = pltpu.make_async_copy(target, tgt.at[c], loc_sem.at[2])
    load_own = pltpu.make_async_copy(hidden.at[:, my_cols], hid.at[c], loc_sem.at[3])
    load_tgt.start()
    load_hfull.start()
    load_own.start()

    barrier = pltpu.get_barrier_semaphore()
    peers = [sib, pair(0), pair(1), zo(0), zo(1), flip] + [xn(k) for k in (1, 2, 3)] + [yn(k) for k in (1, 2, 3)]
    for peer in peers:
        pl.semaphore_signal(barrier, inc=1, device_id=peer, device_id_type=MESH)
    pl.semaphore_wait(barrier, len(peers))

    def piece(half, k):
        place = ((x if half == 0 else y) + k) % 4
        return pl.ds(pl.multiple_of(half * 64 + place * 16, 16), 16)

    go(hidden.at[:, cols_of(2 * zl + 1 - c)], hid.at[c], hs_s.at[0], hs_r.at[c], sib)
    for core in range(2):
        for half in range(2):
            rows = piece(half, 0)
            go(
                hidden.at[rows, cols_of(2 * (1 - zl) + core)], hid.at[2 + c, rows, :],
                fs_s.at[core, half], fs_r.at[c, half], zo(core),
            )
    load_tgt.wait()
    go(tgt.at[c], tgt.at[2 + c], ts_s.at[1], ts_r.at[2 + c], pair(c))
    go(tgt.at[c], tgt.at[c], ts_s.at[0], ts_r.at[c], sib)
    load_head.start()

    load_hfull.wait()

    def sums(i, carry):
        rows = sixteen(i)
        squares = jnp.zeros((ROWS, 1), F32)
        dots = jnp.zeros((ROWS, 1), F32)
        for q in range(8):
            cols = pl.ds(q * 1024, 1024)
            inputs = hfull[rows, cols].astype(F32) + steer[:, cols]
            squares += jnp.sum(inputs * inputs, axis=1, keepdims=True)
            dots += jnp.sum(inputs * tangent[:, cols], axis=1, keepdims=True)
        sq[rows, :] = lanes([squares, dots])
        return carry

    lax.fori_loop(0, 128 // ROWS, sums, 0)
    stats_in[c] = sq[...].T[0:8, :]
    for place, dev in enumerate((sib, zo(0), zo(1))):
        slot = c if place == 0 else 2 + c
        go(stats_in.at[c], stats_in.at[slot], ss_s.at[place], ss_r.at[slot], dev)

    def hop(half, k):
        return xn(k) if half == 0 else yn(k)

    def ring_start():
        for core in range(2):
            for half in range(2):
                ref = hid.at[2 + core, piece(half, 0), :]
                recv(ref, fs_s.at[core, half], fs_r.at[core, half])
                for way in range(2):
                    go(ref, ref, hr_s.at[core, half, way], hr_r.at[core, half, way], hop(half, 1 + 2 * way))

    def ring_relay():
        for core in range(2):
            for half in range(2):
                for way in range(2):
                    rows = piece(half, 3 - 2 * way)
                    recv(hid.at[2 + core, rows, :], hr_s.at[core, half, way], hr_r.at[core, half, way])
                    ref = hid.at[2 + core, rows, way * 1024 : (way + 1) * 1024]
                    go(ref, ref, hr_s.at[core, half, 2 + way], hr_r.at[core, half, 2 + way], hop(half, 1 + 2 * way))

    def ring_end(core):
        for half in range(2):
            for way in range(2):
                ref = hid.at[2 + core, piece(half, 2), way * 1024 : (way + 1) * 1024]
                recv(ref, hr_s.at[core, half, 2 + way], hr_r.at[core, half, 2 + way])

    steer_part = steer[:, my_cols]
    gain_part = gain[:, my_cols]

    def norm_block(p, dest, base):
        sq[...] = jnp.zeros((128, 128), F32)
        sq[0:8, :] = stats_in[p]
        sq[...] = sq[...].T

        def rows_of(i, carry):
            rows = sixteen(i)
            both = sq[rows, :]
            denominator = both[:, 0:1] / full + EPSILON
            inverse = 1.0 / jnp.sqrt(denominator)
            norm_col[i % 2, p, sixteen(i // 2), :] = lanes([inverse, both[:, 1:2] / full / denominator])
            inputs = hid[p, rows, :].astype(F32) + steer_part
            dest[pl.ds(pl.multiple_of((i % 2) * 128 + base + (i // 2) * ROWS, ROWS), ROWS), :] = (gain_part * inputs * inverse).astype(BF16)
            return carry

        lax.fori_loop(0, 128 // ROWS, rows_of, 0)

    product = gain_part * tangent[:, my_cols]
    high = product.astype(BF16).astype(F32)
    row = lax.broadcasted_iota(jnp.int32, (16, depth), 0)
    nrm_loc[256:272, :] = jnp.where(row == 0, high, jnp.where(row == 1, product - high, 0.0)).astype(BF16)

    load_own.wait()
    recv(hid.at[other], hs_s.at[0], hs_r.at[other])
    recv(stats_in.at[other], ss_s.at[0], ss_r.at[other])
    norm_block(0, nrm_loc, 0)
    norm_block(1, nrm_loc, 64)
    ring_start()
    load_head.wait()

    tiles = [(0, 512), (512, 512), (1024, 512), (1536, 512), (2048, 384)]

    def send_codes(half, z, t):
        cols = slice(tiles[t][0], tiles[t][0] + tiles[t][1])
        go(
            code_out.at[half, z, :, cols], code_in.at[z, 2 - 2 * half + c, :, cols],
            cs_s.at[half, z, t], cs_r.at[half, z, t], pair(c),
        )

    def forward(half):
        p0 = 2 * half

        def finish(t):
            start, size = tiles[t]
            cols = slice(start, start + size)
            recv(psib.at[:, p0 + c, :, cols], ps_s.at[half, t], ps_r.at[half, t])

            def rows_of(i, carry):
                rows = sixteen(i // 2)
                z = i % 2
                value = part[z, p0 + c, rows, cols] + psib[z, p0 + c, rows, cols]
                psib[z, p0 + c, rows, cols] = value
                code_out[half, z, rows, cols] = encode(value)
                return carry

            lax.fori_loop(0, 128 // ROWS, rows_of, 0)
            send_codes(half, 0, t)

        for t, (start, size) in enumerate(tiles):
            cols = slice(start, start + size)
            lhs = nrm_loc if half == 0 else nrm_rem
            got = jnp.dot(lhs[...], head[:, cols], preferred_element_type=F32)
            for z in range(2):
                for p in range(2):
                    first = z * 128 + p * 64
                    part[z, p0 + p, :, cols] = got[first : first + 64]
            if half == 0:
                upart[s, :, cols] = jnp.sum(got[256:272], axis=0, keepdims=True)
            rc(
                part.at[:, p0 + other, :, cols], psib.at[:, p0 + other, :, cols],
                ps_s.at[half, t], ps_r.at[half, t], sib,
            ).start()
            if t:
                finish(t - 1)
        finish(len(tiles) - 1)

    g1 = Reduce(ring_of(0), gsb, gr1, ga_s, ga_r)
    g2 = Reduce(ring_of(1), gs2, gr2, gb_s, gb_r)
    m1 = Reduce(ring_of(0), sb, r1, a_s, a_r)
    m2 = Reduce(ring_of(1), s2, r2, b_s, b_r)

    def store(buffer, n, o, p, k, value):
        for h in range(2):
            cols = slice(h * 128, (h + 1) * 128)
            buffer[0, n, h, k, o, pl.ds(p * 32, 32), :] = value[0][:, cols].astype(BF16)
            buffer[1, n, h, p, o, pl.ds(k * 32, 32), :] = value[1][:, cols].astype(BF16)

    def target_chunk(p0, n):
        block = head[pl.ds(pl.multiple_of(n * 512, 512), 512), :]
        got = lax.dot_general(tgt[p0 : p0 + 2].reshape(256, width), block, NT, preferred_element_type=F32)
        for p in range(2):
            for k in range(4):
                rows = got[p * 128 + k * 32 : p * 128 + k * 32 + 32]
                store(gsb, n, 0, p0 + p, k, (rows[:, 0:256], rows[:, 256:512]))

    def target_near(n, carry):
        target_chunk(0, n)
        return carry

    def target_far(n, carry):
        target_chunk(2, n)
        g1.send(n)
        return carry

    forward(0)
    for place, dev in enumerate((sib, pair(0), pair(1))):
        go(upart.at[s], upart.at[s], us_s.at[place], us_r.at[s], dev)
    ring_relay()
    recv(tgt.at[other], ts_s.at[0], ts_r.at[other])
    lax.fori_loop(0, 4, target_near, 0)
    for core in range(2):
        ring_end(core)
        recv(stats_in.at[2 + core], ss_s.at[1], ss_r.at[2 + core])
        norm_block(2 + core, nrm_rem, 64 * core)
    forward(1)
    for half in range(2):
        for t, (start, size) in enumerate(tiles):
            send_codes(half, 1, t)
            ref = part.at[:, 2 * half + other, :, start : start + size]
            rc(ref, ref, ps_s.at[half, t], ps_r.at[half, t], sib).wait_send()

    recv(tgt.at[2 + c], ts_s.at[1], ts_r.at[2 + c])
    go(tgt.at[2 + c], tgt.at[2 + c], tf_s.at[0], tf_r.at[c], sib)
    recv(tgt.at[2 + other], tf_s.at[0], tf_r.at[other])
    lax.fori_loop(0, 4, target_far, 0)

    recv(upart.at[2 * zl + other], us_s.at[0], us_r.at[2 * zl + other])
    for core in range(2):
        recv(upart.at[2 * (1 - zl) + core], us_s.at[1], us_r.at[2 * (1 - zl) + core])
    uvec[...] = (upart[0] + upart[1]) + (upart[2] + upart[3])

    def softmax_rows(z, p):
        def rows_of(i, carry):
            rows = sixteen(i)
            logits = psib[z, p, rows, :] + decode(code_in[z, p, rows, :])
            peak = jnp.max(logits, axis=1, keepdims=True)
            columns = norm_col[z, p, rows, :]
            inverse, along = columns[:, 0:1], columns[:, 1:2]
            u = uvec[...]
            exponent = jnp.exp(logits - peak)
            dlogits = u * inverse - along * logits
            total = jnp.sum(exponent, axis=1, keepdims=True)
            shift = jnp.sum(exponent * dlogits, axis=1, keepdims=True)
            first = jnp.sum(exponent * logits, axis=1, keepdims=True)
            weights = tgt[p, pl.ds(pl.multiple_of(i * 32 + z * 16, 16), 16), :].astype(F32)
            weight_total = jnp.sum(weights, axis=1, keepdims=True)
            weight_first = jnp.sum(weights * logits, axis=1, keepdims=True)
            mean = shift / total
            weighted = exponent * (dlogits - mean)
            second = jnp.sum(weighted * logits, axis=1, keepdims=True) + mean * first
            ef[z, 0, p, rows, :] = exponent.astype(BF16)
            ef[z, 1, p, rows, :] = weighted.astype(BF16)
            st_col[z, p // 2, pl.ds(pl.multiple_of((p % 2) * 64 + i * 16, 16), 16), :] = lanes(
                [peak, total, shift, first, second, weight_total, weight_first]
            )
            return carry

        lax.fori_loop(0, 64 // ROWS, rows_of, 0)

    def softmax(z):
        for half in range(2):
            p = 2 - 2 * half + c
            for t, (start, size) in enumerate(tiles):
                recv(code_in.at[z, p, :, start : start + size], cs_s.at[half, z, t], cs_r.at[half, z, t])
            softmax_rows(z, p)
            go(ef.at[z, :, p], ef.at[z, :, p], cf_s.at[z, half], cf_r.at[z, half], sib)
        mine = pl.ds(pl.multiple_of(c * 64, 64), 64)
        go(st_col.at[z, :, mine, :], st_col.at[z, :, mine, :], cf_s.at[z, 2], cf_r.at[z, 2], sib)
        recv(st_col.at[z, :, pl.ds(pl.multiple_of(other * 64, 64), 64), :], cf_s.at[z, 2], cf_r.at[z, 2])
        for pp in range(2):
            st_in[z, 10, pp] = st_col[z, pp].T[0:8, :]

    def sibling_rows(z):
        for half in range(2):
            recv(ef.at[z, :, 2 - 2 * half + other], cf_s.at[z, half], cf_r.at[z, half])

    def products(z, n):
        cols = pl.ds(pl.multiple_of(n * 512, 512), 512)
        block = head[cols, :]
        got = lax.dot_general(ef[z].reshape(512, width), block, NT, preferred_element_type=F32)
        for p in range(4):
            part[z, p, :, cols] = got[p * 64 : (p + 1) * 64]
            psib[z, p, :, cols] = got[256 + p * 64 : 256 + (p + 1) * 64]

    def merge(a, b):
        peak = jnp.maximum(a[:, 0:1], b[:, 0:1])
        place = lax.broadcasted_iota(jnp.int32, (2, 8, 128), 1)
        scale_a = jnp.where(place < 5, jnp.exp(a[:, 0:1] - peak), 1.0)
        scale_b = jnp.where(place < 5, jnp.exp(b[:, 0:1] - peak), 1.0)
        return jnp.where(place == 0, peak, a * scale_a + b * scale_b)

    def share(z, source, first, step):
        for k in (1, 2, 3):
            slot = first + k - 1
            go(st_in.at[z, source], st_in.at[z, slot], xs_s.at[z, slot], xs_r.at[z, slot], step(k))

    def gather(z, source, first):
        total = st_in[z, source]
        for k in (1, 2, 3):
            slot = first + k - 1
            recv(st_in.at[z, slot], xs_s.at[z, slot], xs_r.at[z, slot])
            total = merge(total, st_in[z, slot])
        return total

    def columns_of(lines, dest):
        sq[...] = jnp.zeros((128, 128), F32)
        for place, line in enumerate(lines):
            sq[place : place + 1, :] = line
        dest[...] = sq[...].T

    def factors(mine, whole):
        factor = jnp.exp(mine[0:1] - whole[0:1])
        return [factor, factor * (mine[2:3] / mine[1:2] - whole[2:3] / whole[1:2])]

    def first_totals(z):
        st_in[z, 11] = gather(z, 10, 0)
        share(z, 11, 6, yn)
        st_in[z, 12] = gather(z, 10, 3)
        for pp in range(2):
            own = st_in[z, 10, pp]
            columns_of(factors(own, st_in[z, 11, pp]) + factors(own, st_in[z, 12, pp]), fin_col.at[pp])
        for p in range(4):
            columns = fin_col[p // 2, (p % 2) * 64 : (p % 2) * 64 + 64, :]
            for kind in range(4):
                wide[kind, p] = jnp.broadcast_to(columns[:, kind : kind + 1], (64, 128))

    def second_totals(z):
        st_in[z, 13] = gather(z, 11, 6)
        go(st_in.at[z, 13], st_in.at[z, 9], xs_s.at[z, 9], xs_r.at[z, 9], flip)
        for pp in range(2):
            both = st_in[z, 13, pp]
            columns_of(factors(st_in[z, 11, pp], both) + factors(st_in[z, 12, pp], both), fin2.at[z, pp])

    def first_stage(z):
        def chunk(n, carry):
            place = z * 4 + n
            for p in range(4):
                for route in range(2):
                    factor, turn = wide[2 * route, p], wide[2 * route + 1, p]
                    for h in range(2):
                        cols = pl.ds(pl.multiple_of(n * 512 + route * 256 + h * 128, 128), 128)
                        value = part[z, p, :, cols]
                        scaled = (factor * value).astype(BF16)
                        weighted = (factor * psib[z, p, :, cols] + turn * value).astype(BF16)
                        for o, rows in enumerate((scaled, weighted)):
                            if route == 1:
                                sb[1, place, h, p, o] = rows
                            else:
                                for k in range(4):
                                    sb[0, place, h, k, o, pl.ds(p * 16, 16), :] = rows[k * 16 : (k + 1) * 16]
            m1.send(place)

            @pl.when(n < 3)
            def _():
                products(z, n + 1)

            @pl.when(n > 0)
            def _():
                m1.relay(place - 1)

            return carry

        lax.fori_loop(0, 4, chunk, 0)

    def second_stage(z):
        def chunk(n, carry):
            place = z * 4 + n
            m1.wait(place)
            for route in range(2):
                for h in range(2):
                    for d in range(4):
                        rows = pl.ds(d * 16, 16)
                        if route == 0:
                            columns = fin2[z, d // 2, pl.ds(pl.multiple_of((d % 2) * 64 + x * 16, 16), 16), :][:, 0:2]
                        else:
                            here = pl.ds(pl.multiple_of((p_mine % 2) * 64 + d * 16, 16), 16)
                            columns = fin2[z, p_mine // 2, here, :][:, 2:4]
                        e_sum = m1.total(route, place, h, 0, rows)
                        f_sum = m1.total(route, place, h, 1, rows)
                        s2[route, place, h, d, 0] = (columns[:, 0:1] * e_sum).astype(BF16)
                        s2[route, place, h, d, 1] = (columns[:, 0:1] * f_sum + columns[:, 1:2] * e_sum).astype(BF16)
            m2.send(place)
            return carry

        lax.fori_loop(0, 4, chunk, 0)

    def last_copy(sent, landed, ssem, rsem, place, n):
        return rc(sent.at[place], landed.at[n], ssem.at[n], rsem.at[n], flip)

    def main_last(z):
        def chunk(n, carry):
            place = z * 4 + n
            m2.wait(place)
            for route in range(2):
                for h in range(2):
                    for o in range(2):
                        value = m2.total(route, place, h, o, pl.ds(0, 16))
                        t2[place, o, :, route * 256 + h * 128 : route * 256 + h * 128 + 128] = value

            @pl.when(zh != z)
            def _():
                s3[place] = t2[place].astype(BF16)
                last_copy(s3, r3, z_s, z_r, place, n).start()

            return carry

        lax.fori_loop(0, 4, chunk, 0)

    def target_second(n, carry):
        g1.wait(n)
        for route in range(2):
            for h in range(2):
                for d in range(4):
                    gs2[route, n, h, d, 0] = g1.total(route, n, h, 0, pl.ds(d * 32, 32)).astype(BF16)
        g2.send(n)
        return carry

    def target_last(n, carry):
        g2.wait(n)
        for route in range(2):
            for h in range(2):
                value = g2.total(route, n, h, 0, pl.ds(0, 32))
                for z in range(2):
                    gt2[n, 0, z, :, route * 256 + h * 128 : route * 256 + h * 128 + 128] = value[z * 16 : (z + 1) * 16]
        gs3[n, 0] = gt2[n, 0, 1 - zh].astype(BF16)
        last_copy(gs3, gr3, gz_s, gz_r, n, n).start()
        return carry

    def relays(reduce, first):
        def one(n, carry):
            reduce.relay(first + n)
            return carry

        lax.fori_loop(0, 4, one, 0)

    softmax(0)
    share(0, 10, 0, xn)
    share(0, 10, 3, yn)
    relays(g1, 0)
    sibling_rows(0)
    products(0, 0)
    first_totals(0)
    first_stage(0)
    lax.fori_loop(0, 4, target_second, 0)
    second_totals(0)
    m1.relay(3)

    softmax(1)
    share(1, 10, 0, xn)
    share(1, 10, 3, yn)
    second_stage(0)
    sibling_rows(1)
    products(1, 0)
    first_totals(1)
    relays(m2, 0)
    first_stage(1)
    relays(g2, 0)
    second_totals(1)
    m1.relay(7)
    main_last(0)
    second_stage(1)
    lax.fori_loop(0, 4, target_last, 0)
    g1.drain()
    m1.drain()
    relays(m2, 4)
    g2.drain()
    for copy in sends:
        copy.wait_send()

    for z in range(2):
        recv(st_in.at[z, 9], xs_s.at[z, 9], xs_r.at[z, 9])
    st_in[zh, 14] = merge(st_in[zh, 13], st_in[zh, 9])
    whole = st_in[zh, 14, p_mine // 2]
    shift = whole[2:3] / whole[1:2]
    mean_logit = whole[3:4] / whole[1:2]
    lines = []
    for slot in (13, 9):
        lines += [line / whole[1:2] for line in factors(st_in[zh, slot, p_mine // 2], whole)]
    weight = 1.0 / whole[5:6]
    lines += [weight, mean_logit - whole[6:7] * weight, whole[4:5] / whole[1:2] - shift * mean_logit]
    columns_of(lines, fin3)

    main_last(1)

    rows = pl.ds(pl.multiple_of(x * 32 + zh * 16, 16), 16)
    norms = norm_col[zh, p_mine, pl.ds(pl.multiple_of(x * 16, 16), 16), :]
    inverse = norms[:, 0:1]
    out_col[...] = norms
    columns = fin3[pl.ds(pl.multiple_of((p_mine % 2) * 64 + x * 16, 16), 16), :]

    def column(place):
        return columns[:, place : place + 1]

    def finish_chunk(n, carry):
        cols = pl.ds(pl.multiple_of(n * 512, 512), 512)
        far = pl.ds(pl.multiple_of(s * depth + n * 512, 512), 512)
        last_copy(gs3, gr3, gz_s, gz_r, n, n).wait_recv()
        last_copy(s3, r3, z_s, z_r, n, n).wait_recv()
        inputs = hid[p_mine, rows, cols].astype(F32) + steer[:, far]
        place = zh * 4 + n
        e_own, e_far = t2[place, 0], r3[n, 0].astype(F32)
        f_own, f_far = t2[place, 1], r3[n, 1].astype(F32)
        targets = gt2[n, 0, zh] + gr3[n, 0].astype(F32)
        grad = column(0) * e_own + column(2) * e_far - column(4) * targets
        ggn = column(0) * f_own + column(1) * e_own + column(2) * f_far + column(3) * e_far
        for o, back in enumerate((grad, ggn)):
            slope = column(5 + o) * inverse * (1.0 / full)
            out[o, :, cols] = gain[:, far] * back - inputs * slope
        return carry

    lax.fori_loop(0, 4, finish_chunk, 0)

    m2.drain()
    for n in range(4):
        last_copy(gs3, gr3, gz_s, gz_r, n, n).wait_send()
        last_copy(s3, r3, z_s, z_r, n, n).wait_send()


def body(hidden, steer, tangent, gain, head, target):
    vmem = pltpu.VMEM
    dma = pltpu.SemaphoreType.DMA
    any_spec = pl.BlockSpec(memory_space=pl.ANY)
    vmem_spec = pl.BlockSpec(memory_space=pltpu.VMEM)
    result, columns = pl.pallas_call(
        kernel,
        out_shape=[jax.ShapeDtypeStruct((2, 16, 2048), F32), jax.ShapeDtypeStruct((16, 128), F32)],
        in_specs=[any_spec] * 3 + [vmem_spec] * 3,
        out_specs=[vmem_spec] * 2,
        scratch_shapes=[
            vmem((128, 8192), BF16),
            vmem((4, 128, 2048), BF16),
            vmem((4, 8, 128), F32),
            vmem((128, 128), F32),
            vmem((2048, 2432), BF16),
            vmem((272, 2048), BF16),
            vmem((256, 2048), BF16),
            vmem((4, 1, 2432), F32),
            vmem((1, 2432), F32),
            vmem((2, 4, 64, 2432), F32),
            vmem((2, 4, 64, 2432), F32),
            vmem((2, 2, 64, 2432), BF16),
            vmem((2, 4, 64, 2432), BF16),
            vmem((4, 128, 2432), BF16),
            vmem((2, 2, 4, 64, 2432), BF16),
            vmem((2, 4, 64, 128), F32),
            vmem((2, 2, 128, 128), F32),
            vmem((2, 15, 2, 8, 128), F32),
            vmem((2, 128, 128), F32),
            vmem((4, 4, 64, 128), F32),
            vmem((2, 2, 128, 128), F32),
            vmem((128, 128), F32),
            vmem((2, 8, 2, 4, 2, 64, 128), BF16),
            vmem((2, 8, 2, 3, 2, 64, 128), BF16),
            vmem((2, 8, 2, 4, 2, 16, 128), BF16),
            vmem((2, 8, 2, 3, 2, 16, 128), BF16),
            vmem((8, 2, 16, 512), F32),
            vmem((8, 2, 16, 512), BF16),
            vmem((4, 2, 16, 512), BF16),
            vmem((2, 4, 2, 4, 1, 128, 128), BF16),
            vmem((2, 4, 2, 3, 1, 128, 128), BF16),
            vmem((2, 4, 2, 4, 1, 32, 128), BF16),
            vmem((2, 4, 2, 3, 1, 32, 128), BF16),
            vmem((4, 1, 2, 16, 512), F32),
            vmem((4, 1, 16, 512), BF16),
            vmem((4, 1, 16, 512), BF16),
            dma((4,)),
            dma((1,)), dma((4,)),
            dma((2, 2)), dma((2, 2)),
            dma((2, 2, 4)), dma((2, 2, 4)),
            dma((3,)), dma((4,)),
            dma((3,)), dma((4,)),
            dma((2,)), dma((4,)),
            dma((1,)), dma((2,)),
            dma((2, 5)), dma((2, 5)),
            dma((2, 2, 5)), dma((2, 2, 5)),
            dma((2, 3)), dma((2, 3)),
            dma((2, 10)), dma((2, 10)),
            dma((1,)), dma((8, 2)),
            dma((1,)), dma((8, 2)),
            dma((4,)), dma((4,)),
            dma((1,)), dma((4, 2)),
            dma((1,)), dma((4, 2)),
            dma((4,)), dma((4,)),
        ],
        compiler_params=pltpu.CompilerParams(
            collective_id=0, has_side_effects=True, vmem_limit_bytes=64 * 1024 * 1024 - 65536
        ),
    )(hidden, head, target, steer.reshape(1, -1), tangent.reshape(1, -1), gain.reshape(1, -1))
    inverse = columns[:, 0:1]
    return result[0] * inverse, result[1] * inverse


def solution(mesh):
    return jax.shard_map(
        body,
        mesh=mesh,
        in_specs=(P("seq", None), P(), P(), P(), P("seq", "vocab"), P("seq", "vocab")),
        out_specs=(P("vocab", "seq"), P("vocab", "seq")),
        check_vma=False,
    )
```

```python
import jax
import jax.numpy as jnp
from jax import lax
from jax.experimental import pallas as pl
from jax.experimental.pallas import tpu as pltpu
from jax.sharding import PartitionSpec as P

EPSILON = 1e-06
MESH = pl.DeviceIdType.MESH
F32 = jnp.float32
BF16 = jnp.bfloat16
NT = (((1,), (1,)), ((), ()))
ROWS = 16
KNEE = 8.0
POWER = 32
SHIFT = 126.0 / POWER


def encode(value):
    code = (1.0 + jnp.abs(value) * (1.0 / KNEE)) * (2.0**-SHIFT)
    for _ in range(5):
        code = code * code
    return jnp.where(value < 0, -code, code).astype(BF16)


def decode(code):
    code = code.astype(F32)
    root = jnp.exp2(jnp.log2(jnp.abs(code)) * (1.0 / POWER) + SHIFT)
    size = (root - 1.0) * KNEE
    return jnp.where(code < 0, -size, size)


def lanes(columns):
    rows = columns[0].shape[0]
    lane = lax.broadcasted_iota(jnp.int32, (rows, 128), 1)
    out = jnp.zeros((rows, 128), F32)
    for place, column in enumerate(columns):
        out = jnp.where(lane == place, column, out)
    return out


class Reduce:
    def __init__(self, ring, buffer, landing, send_sem, recv_sem):
        self.ring, self.buffer, self.landing = ring, buffer, landing
        self.send_sem, self.recv_sem = send_sem, recv_sem

    def copies(self, route, n):
        right, left, at = self.ring(route)

        def copy(h, kind, dest, device):
            return pltpu.make_async_remote_copy(
                src_ref=self.buffer.at[route, n, h, dest],
                dst_ref=self.landing.at[route, n, h, kind],
                send_sem=self.send_sem.at[0],
                recv_sem=self.recv_sem.at[n, min(kind, 1)],
                device_id=device,
                device_id_type=MESH,
            )

        opposite = [copy(0, 0, at(2), right), copy(1, 0, at(2), left)]
        raw = [copy(0, 1, at(3), left), copy(1, 1, at(1), right)]
        summed = [copy(0, 2, at(1), right), copy(1, 2, at(3), left)]
        return at, opposite, raw, summed

    def send(self, n):
        for route in range(2):
            _, opposite, raw, _ = self.copies(route, n)
            for copy in opposite + raw:
                copy.start()

    def all_of(self, ref, recv_sem):
        return pltpu.make_async_remote_copy(
            src_ref=ref, dst_ref=ref, send_sem=self.send_sem.at[0], recv_sem=recv_sem,
            device_id=self.ring(0)[0], device_id_type=MESH,
        )

    def relay(self, n):
        self.all_of(self.landing.at[:, n, :, 0], self.recv_sem.at[n, 0]).wait_recv()
        for route in range(2):
            at, _, _, summed = self.copies(route, n)
            for h in range(2):
                where = at(1) if h == 0 else at(3)
                mine = self.buffer[route, n, h, where].astype(F32)
                self.buffer[route, n, h, where] = (mine + self.landing[route, n, h, 0].astype(F32)).astype(BF16)
                summed[h].start()

    def wait(self, n):
        self.all_of(self.landing.at[:, n, :, 1:3], self.recv_sem.at[n, 1]).wait_recv()

    def total(self, route, n, h, o, rows):
        at = self.ring(route)[2]
        out = self.buffer[route, n, h, at(0), o, rows, :].astype(F32)
        return out + self.landing[route, n, h, 1, o, rows, :].astype(F32) + self.landing[route, n, h, 2, o, rows, :].astype(F32)

    def drain(self):
        self.all_of(self.landing, self.recv_sem.at[0, 0]).wait_send()


def kernel(
    hidden, head_hbm, target, steer, tangent, gain,
    out, out_sub,
    hfull, hid, stats_in, sq, head, nrm_loc, nrm_rem, upart, uvec, part, psib, code_out, code_in, tgt,
    ef, norm_col, st_col, st_in, fin_col, wide, fin2, fin3,
    sb, r1, s2, r2, t2, s3, r3, gsb, gr1, gs2, gr2, gt2, gs3, gr3,
    loc_sem, hs_s, hs_r, fs_s, fs_r, hr_s, hr_r, ss_s, ss_r, us_s, us_r, ts_s, ts_r, tf_s, tf_r, ps_s, ps_r,
    cs_s, cs_r, cf_s, cf_r, xs_s, xs_r, a_s, a_r, b_s, b_r, z_s, z_r, ga_s, ga_r, gb_s, gb_r, gz_s, gz_r,
):
    s = lax.axis_index("seq")
    v = lax.axis_index("vocab")
    zl, c = s // 2, s % 2
    y, x, zh = v // 8, (v // 2) % 4, v % 2
    depth = 2048
    width = 2432
    full = 8192
    other = 1 - c
    p_mine = (y + 2 * zl) % 4
    sib = {"seq": 2 * zl + 1 - c, "vocab": v}
    flip = {"seq": s, "vocab": v + 1 - 2 * zh}

    def pair(core):
        return {"seq": 2 * (1 - zl) + core, "vocab": v}

    def zo(core):
        return {"seq": 2 * (1 - zl) + core, "vocab": v + 1 - 2 * zh}

    def xn(k):
        return {"seq": s, "vocab": y * 8 + ((x + k) % 4) * 2 + zh}

    def yn(k):
        return {"seq": s, "vocab": ((y + k) % 4) * 8 + x * 2 + zh}

    def ring_of(stage):
        def ring(route):
            if route == stage:
                return xn(1), xn(3), lambda k: (x + k) % 4
            return yn(1), yn(3), lambda k: (y + k + 2 * zl) % 4

        return ring

    def rc(src, dst, ssem, rsem, dev):
        return pltpu.make_async_remote_copy(
            src_ref=src, dst_ref=dst, send_sem=ssem, recv_sem=rsem, device_id=dev, device_id_type=MESH
        )

    sends = []

    def go(*args):
        copy = rc(*args)
        copy.start()
        sends.append(copy)

    def recv(dst, ssem, rsem):
        rc(dst, dst, ssem, rsem, sib).wait_recv()

    def cols_of(seq):
        return pl.ds(pl.multiple_of(seq * depth, depth), depth)

    def sixteen(i):
        return pl.ds(pl.multiple_of(i * ROWS, ROWS), ROWS)

    my_cols = cols_of(s)
    load_head = pltpu.make_async_copy(head_hbm, head, loc_sem.at[0])
    load_hfull = pltpu.make_async_copy(hidden, hfull, loc_sem.at[1])
    load_tgt = pltpu.make_async_copy(target, tgt.at[c], loc_sem.at[2])
    load_own = pltpu.make_async_copy(hidden.at[:, my_cols], hid.at[c], loc_sem.at[3])
    load_tgt.start()
    load_hfull.start()
    load_own.start()

    barrier = pltpu.get_barrier_semaphore()
    peers = [sib, pair(0), pair(1), zo(0), zo(1), flip] + [xn(k) for k in (1, 2, 3)] + [yn(k) for k in (1, 2, 3)]
    for peer in peers:
        pl.semaphore_signal(barrier, inc=1, device_id=peer, device_id_type=MESH)
    steer_part = steer[:, my_cols]
    gain_part = gain[:, my_cols]
    product = gain_part * tangent[:, my_cols]
    high = product.astype(BF16).astype(F32)
    row = lax.broadcasted_iota(jnp.int32, (16, depth), 0)
    nrm_loc[256:272, :] = jnp.where(row == 0, high, jnp.where(row == 1, product - high, 0.0)).astype(BF16)

    load_hfull.wait()

    def sums(i, carry):
        rows = sixteen(i)
        squares = jnp.zeros((ROWS, 1), F32)
        dots = jnp.zeros((ROWS, 1), F32)
        for q in range(8):
            cols = pl.ds(q * 1024, 1024)
            inputs = hfull[rows, cols].astype(F32) + steer[:, cols]
            squares += jnp.sum(inputs * inputs, axis=1, keepdims=True)
            dots += jnp.sum(inputs * tangent[:, cols], axis=1, keepdims=True)
        sq[rows, :] = lanes([squares, dots])
        return carry

    lax.fori_loop(0, 128 // ROWS, sums, 0)
    stats_in[c] = sq[...].T[0:8, :]
    pl.semaphore_wait(barrier, len(peers))

    def piece(half, k):
        place = ((x if half == 0 else y) + k) % 4
        return pl.ds(pl.multiple_of(half * 64 + place * 16, 16), 16)

    for place, dev in enumerate((sib, zo(0), zo(1))):
        slot = c if place == 0 else 2 + c
        go(stats_in.at[c], stats_in.at[slot], ss_s.at[place], ss_r.at[slot], dev)
    go(hidden.at[:, cols_of(2 * zl + 1 - c)], hid.at[c], hs_s.at[0], hs_r.at[c], sib)
    for core in range(2):
        for half in range(2):
            rows = piece(half, 0)
            go(
                hidden.at[rows, cols_of(2 * (1 - zl) + core)], hid.at[2 + c, rows, :],
                fs_s.at[core, half], fs_r.at[c, half], zo(core),
            )
    load_tgt.wait()
    go(tgt.at[c], tgt.at[2 + c], ts_s.at[1], ts_r.at[2 + c], pair(c))
    go(tgt.at[c], tgt.at[c], ts_s.at[0], ts_r.at[c], sib)
    load_head.start()

    def hop(half, k):
        return xn(k) if half == 0 else yn(k)

    def ring_start():
        for core in range(2):
            for half in range(2):
                ref = hid.at[2 + core, piece(half, 0), :]
                recv(ref, fs_s.at[core, half], fs_r.at[core, half])
                for way in range(2):
                    go(ref, ref, hr_s.at[core, half, way], hr_r.at[core, half, way], hop(half, 1 + 2 * way))

    def ring_relay():
        for core in range(2):
            for half in range(2):
                for way in range(2):
                    rows = piece(half, 3 - 2 * way)
                    recv(hid.at[2 + core, rows, :], hr_s.at[core, half, way], hr_r.at[core, half, way])
                    ref = hid.at[2 + core, rows, way * 1024 : (way + 1) * 1024]
                    go(ref, ref, hr_s.at[core, half, 2 + way], hr_r.at[core, half, 2 + way], hop(half, 1 + 2 * way))

    def ring_end(core):
        for half in range(2):
            for way in range(2):
                ref = hid.at[2 + core, piece(half, 2), way * 1024 : (way + 1) * 1024]
                recv(ref, hr_s.at[core, half, 2 + way], hr_r.at[core, half, 2 + way])


    def norm_block(p, dest, base):
        sq[...] = jnp.zeros((128, 128), F32)
        sq[0:8, :] = stats_in[p]
        sq[...] = sq[...].T

        def rows_of(i, carry):
            rows = sixteen(i)
            both = sq[rows, :]
            denominator = both[:, 0:1] / full + EPSILON
            inverse = 1.0 / jnp.sqrt(denominator)
            norm_col[i % 2, p, sixteen(i // 2), :] = lanes([inverse, both[:, 1:2] / full / denominator])
            inputs = hid[p, rows, :].astype(F32) + steer_part
            dest[pl.ds(pl.multiple_of((i % 2) * 128 + base + (i // 2) * ROWS, ROWS), ROWS), :] = (gain_part * inputs * inverse).astype(BF16)
            return carry

        lax.fori_loop(0, 128 // ROWS, rows_of, 0)

    load_own.wait()
    recv(hid.at[other], hs_s.at[0], hs_r.at[other])
    recv(stats_in.at[other], ss_s.at[0], ss_r.at[other])
    norm_block(0, nrm_loc, 0)
    norm_block(1, nrm_loc, 64)
    load_head.wait()

    tiles = [(0, 512), (512, 512), (1024, 512), (1536, 512), (2048, 384)]

    def send_codes(half, z, t):
        cols = slice(tiles[t][0], tiles[t][0] + tiles[t][1])
        rc(
            code_out.at[half, z, :, cols], code_in.at[z, 2 - 2 * half + c, :, cols],
            cs_s.at[0], cs_r.at[half, z], pair(c),
        ).start()

    def forward(half):
        p0 = 2 * half

        def finish(t):
            start, size = tiles[t]
            cols = slice(start, start + size)
            recv(psib.at[:, p0 + c, :, cols], ps_s.at[half, t], ps_r.at[half, t])

            def rows_of(i, carry):
                rows = sixteen(i // 2)
                z = i % 2
                value = part[z, p0 + c, rows, cols] + psib[z, p0 + c, rows, cols]
                psib[z, p0 + c, rows, cols] = value
                code_out[half, z, rows, cols] = encode(value)
                return carry

            lax.fori_loop(0, 128 // ROWS, rows_of, 0)
            send_codes(half, 0, t)

        for t, (start, size) in enumerate(tiles):
            cols = slice(start, start + size)
            lhs = nrm_loc if half == 0 else nrm_rem
            got = jnp.dot(lhs[...], head[:, cols], preferred_element_type=F32)
            for z in range(2):
                for p in range(2):
                    first = z * 128 + p * 64
                    part[z, p0 + p, :, cols] = got[first : first + 64]
            if half == 0:
                upart[s, :, cols] = jnp.sum(got[256:272], axis=0, keepdims=True)
            rc(
                part.at[:, p0 + other, :, cols], psib.at[:, p0 + other, :, cols],
                ps_s.at[half, t], ps_r.at[half, t], sib,
            ).start()
            if half == 0 and t == 2:
                ring_start()
            if t:
                finish(t - 1)
        finish(len(tiles) - 1)

    g1 = Reduce(ring_of(0), gsb, gr1, ga_s, ga_r)
    g2 = Reduce(ring_of(1), gs2, gr2, gb_s, gb_r)
    m1 = Reduce(ring_of(0), sb, r1, a_s, a_r)
    m2 = Reduce(ring_of(1), s2, r2, b_s, b_r)

    def store(buffer, n, o, p, k, value):
        for h in range(2):
            cols = slice(h * 128, (h + 1) * 128)
            buffer[0, n, h, k, o, pl.ds(p * 32, 32), :] = value[0][:, cols].astype(BF16)
            buffer[1, n, h, p, o, pl.ds(k * 32, 32), :] = value[1][:, cols].astype(BF16)

    def target_chunk(p0, n):
        block = head[pl.ds(pl.multiple_of(n * 512, 512), 512), :]
        got = lax.dot_general(tgt[p0 : p0 + 2].reshape(256, width), block, NT, preferred_element_type=F32)
        for p in range(2):
            for k in range(4):
                rows = got[p * 128 + k * 32 : p * 128 + k * 32 + 32]
                store(gsb, n, 0, p0 + p, k, (rows[:, 0:256], rows[:, 256:512]))

    def target_near(n, carry):
        target_chunk(0, n)
        return carry

    def target_far(n, carry):
        target_chunk(2, n)
        g1.send(n)
        return carry

    forward(0)
    for place, dev in enumerate((sib, pair(0), pair(1))):
        go(upart.at[s], upart.at[s], us_s.at[place], us_r.at[s], dev)
    recv(tgt.at[other], ts_s.at[0], ts_r.at[other])
    lax.fori_loop(0, 2, target_near, 0)
    ring_relay()
    lax.fori_loop(2, 4, target_near, 0)
    recv(tgt.at[2 + c], ts_s.at[1], ts_r.at[2 + c])
    go(tgt.at[2 + c], tgt.at[2 + c], tf_s.at[0], tf_r.at[c], sib)
    for core in range(2):
        ring_end(core)
        recv(stats_in.at[2 + core], ss_s.at[1], ss_r.at[2 + core])
        norm_block(2 + core, nrm_rem, 64 * core)
    forward(1)
    for half in range(2):
        for t, (start, size) in enumerate(tiles):
            send_codes(half, 1, t)
            ref = part.at[:, 2 * half + other, :, start : start + size]
            rc(ref, ref, ps_s.at[half, t], ps_r.at[half, t], sib).wait_send()

    recv(tgt.at[2 + other], tf_s.at[0], tf_r.at[other])
    lax.fori_loop(0, 4, target_far, 0)

    recv(upart.at[2 * zl + other], us_s.at[0], us_r.at[2 * zl + other])
    for core in range(2):
        recv(upart.at[2 * (1 - zl) + core], us_s.at[1], us_r.at[2 * (1 - zl) + core])
    uvec[...] = (upart[0] + upart[1]) + (upart[2] + upart[3])

    def softmax_rows(z, p):
        def rows_of(i, carry):
            rows = sixteen(i)
            logits = psib[z, p, rows, :] + decode(code_in[z, p, rows, :])
            peak = jnp.max(logits, axis=1, keepdims=True)
            columns = norm_col[z, p, rows, :]
            inverse, along = columns[:, 0:1], columns[:, 1:2]
            u = uvec[...]
            exponent = jnp.exp(logits - peak)
            dlogits = u * inverse - along * logits
            total = jnp.sum(exponent, axis=1, keepdims=True)
            shift = jnp.sum(exponent * dlogits, axis=1, keepdims=True)
            first = jnp.sum(exponent * logits, axis=1, keepdims=True)
            weights = tgt[p, pl.ds(pl.multiple_of(i * 32 + z * 16, 16), 16), :].astype(F32)
            weight_total = jnp.sum(weights, axis=1, keepdims=True)
            weight_first = jnp.sum(weights * logits, axis=1, keepdims=True)
            mean = shift / total
            weighted = exponent * (dlogits - mean)
            second = jnp.sum(weighted * logits, axis=1, keepdims=True) + mean * first
            ef[z, 0, p, rows, :] = exponent.astype(BF16)
            ef[z, 1, p, rows, :] = weighted.astype(BF16)
            st_col[z, p // 2, pl.ds(pl.multiple_of((p % 2) * 64 + i * 16, 16), 16), :] = lanes(
                [peak, total, shift, first, second, weight_total, weight_first]
            )
            return carry

        lax.fori_loop(0, 64 // ROWS, rows_of, 0)

    def softmax(z):
        for half in range(2):
            p = 2 - 2 * half + c
            recv(code_in.at[z, p], cs_s.at[0], cs_r.at[half, z])
            softmax_rows(z, p)
            go(ef.at[z, :, p], ef.at[z, :, p], cf_s.at[z, half], cf_r.at[z, half], sib)
            if z == 1 and half == 0:
                m1.relay(3)
        mine = pl.ds(pl.multiple_of(c * 64, 64), 64)
        go(st_col.at[z, :, mine, :], st_col.at[z, :, mine, :], cf_s.at[z, 2], cf_r.at[z, 2], sib)
        recv(st_col.at[z, :, pl.ds(pl.multiple_of(other * 64, 64), 64), :], cf_s.at[z, 2], cf_r.at[z, 2])
        for pp in range(2):
            st_in[z, 10, pp] = st_col[z, pp].T[0:8, :]

    def sibling_rows(z):
        for half in range(2):
            recv(ef.at[z, :, 2 - 2 * half + other], cf_s.at[z, half], cf_r.at[z, half])

    def products(z, n):
        cols = pl.ds(pl.multiple_of(n * 512, 512), 512)
        block = head[cols, :]
        got = lax.dot_general(ef[z].reshape(512, width), block, NT, preferred_element_type=F32)
        for p in range(4):
            part[z, p, :, cols] = got[p * 64 : (p + 1) * 64]
            psib[z, p, :, cols] = got[256 + p * 64 : 256 + (p + 1) * 64]

    def merge(a, b):
        peak = jnp.maximum(a[:, 0:1], b[:, 0:1])
        place = lax.broadcasted_iota(jnp.int32, (2, 8, 128), 1)
        scale_a = jnp.where(place < 5, jnp.exp(a[:, 0:1] - peak), 1.0)
        scale_b = jnp.where(place < 5, jnp.exp(b[:, 0:1] - peak), 1.0)
        return jnp.where(place == 0, peak, a * scale_a + b * scale_b)

    def share(z, source, first, step):
        for k in (1, 2, 3):
            slot = first + k - 1
            rc(st_in.at[z, source], st_in.at[z, slot], xs_s.at[0], xs_r.at[z, first // 3], step(k)).start()

    def gather(z, source, first):
        recv(st_in.at[z, first : first + 3], xs_s.at[0], xs_r.at[z, first // 3])
        total = st_in[z, source]
        for k in range(3):
            total = merge(total, st_in[z, first + k])
        return total

    def columns_of(lines, dest):
        sq[...] = jnp.zeros((128, 128), F32)
        for place, line in enumerate(lines):
            sq[place : place + 1, :] = line
        dest[...] = sq[...].T

    def factors(mine, whole):
        factor = jnp.exp(mine[0:1] - whole[0:1])
        return [factor, factor * (mine[2:3] / mine[1:2] - whole[2:3] / whole[1:2])]

    def first_totals(z):
        st_in[z, 11] = gather(z, 10, 0)
        share(z, 11, 6, yn)
        st_in[z, 12] = gather(z, 10, 3)
        for pp in range(2):
            own = st_in[z, 10, pp]
            columns_of(factors(own, st_in[z, 11, pp]) + factors(own, st_in[z, 12, pp]), fin_col.at[pp])
        for p in range(4):
            columns = fin_col[p // 2, (p % 2) * 64 : (p % 2) * 64 + 64, :]
            for kind in range(4):
                wide[kind, p] = jnp.broadcast_to(columns[:, kind : kind + 1], (64, 128))

    def second_totals(z):
        st_in[z, 13] = gather(z, 11, 6)
        rc(st_in.at[z, 13], st_in.at[z, 9], xs_s.at[0], xs_r.at[z, 3], flip).start()
        for pp in range(2):
            both = st_in[z, 13, pp]
            columns_of(factors(st_in[z, 11, pp], both) + factors(st_in[z, 12, pp], both), fin2.at[z, pp])

    def first_stage(z):
        def chunk(n, carry):
            place = z * 4 + n
            for p in range(4):
                for route in range(2):
                    factor, turn = wide[2 * route, p], wide[2 * route + 1, p]
                    for h in range(2):
                        cols = pl.ds(pl.multiple_of(n * 512 + route * 256 + h * 128, 128), 128)
                        value = part[z, p, :, cols]
                        scaled = (factor * value).astype(BF16)
                        weighted = (factor * psib[z, p, :, cols] + turn * value).astype(BF16)
                        for o, rows in enumerate((scaled, weighted)):
                            if route == 1:
                                sb[1, place, h, p, o] = rows
                            else:
                                for k in range(4):
                                    sb[0, place, h, k, o, pl.ds(p * 16, 16), :] = rows[k * 16 : (k + 1) * 16]
            m1.send(place)

            @pl.when(n < 2)
            def _():
                products(z, n + 2)

            @pl.when(n > 1)
            def _():
                m1.relay(place - 2)

            return carry

        lax.fori_loop(0, 4, chunk, 0)

    def second_stage(z):
        def chunk(n, carry):
            place = z * 4 + n
            m1.wait(place)
            for route in range(2):
                for h in range(2):
                    for d in range(4):
                        rows = pl.ds(d * 16, 16)
                        if route == 0:
                            columns = fin2[z, d // 2, pl.ds(pl.multiple_of((d % 2) * 64 + x * 16, 16), 16), :][:, 0:2]
                        else:
                            here = pl.ds(pl.multiple_of((p_mine % 2) * 64 + d * 16, 16), 16)
                            columns = fin2[z, p_mine // 2, here, :][:, 2:4]
                        e_sum = m1.total(route, place, h, 0, rows)
                        f_sum = m1.total(route, place, h, 1, rows)
                        s2[route, place, h, d, 0] = (columns[:, 0:1] * e_sum).astype(BF16)
                        s2[route, place, h, d, 1] = (columns[:, 0:1] * f_sum + columns[:, 1:2] * e_sum).astype(BF16)
            m2.send(place)
            return carry

        lax.fori_loop(0, 4, chunk, 0)

    def last_copy(sent, landed, ssem, rsem, place, n):
        return rc(sent.at[place], landed.at[n], ssem.at[n], rsem.at[n], flip)

    def main_last(z):
        def chunk(n, carry):
            place = z * 4 + n
            m2.wait(place)
            for route in range(2):
                for h in range(2):
                    for o in range(2):
                        value = m2.total(route, place, h, o, pl.ds(0, 16))
                        t2[place, o, :, route * 256 + h * 128 : route * 256 + h * 128 + 128] = value

            @pl.when(zh != z)
            def _():
                s3[place] = t2[place].astype(BF16)
                last_copy(s3, r3, z_s, z_r, place, n).start()

            return carry

        lax.fori_loop(0, 4, chunk, 0)

    def target_second(n, carry):
        g1.wait(n)
        for route in range(2):
            for h in range(2):
                for d in range(4):
                    gs2[route, n, h, d, 0] = g1.total(route, n, h, 0, pl.ds(d * 32, 32)).astype(BF16)
        g2.send(n)
        return carry

    def target_last(n, carry):
        g2.wait(n)
        for route in range(2):
            for h in range(2):
                value = g2.total(route, n, h, 0, pl.ds(0, 32))
                for z in range(2):
                    gt2[n, 0, z, :, route * 256 + h * 128 : route * 256 + h * 128 + 128] = value[z * 16 : (z + 1) * 16]
        gs3[n, 0] = gt2[n, 0, 1 - zh].astype(BF16)
        last_copy(gs3, gr3, gz_s, gz_r, n, n).start()
        return carry

    def relays(reduce, first):
        def one(n, carry):
            reduce.relay(first + n)
            return carry

        lax.fori_loop(0, 4, one, 0)

    softmax(0)
    share(0, 10, 0, xn)
    share(0, 10, 3, yn)
    relays(g1, 0)
    sibling_rows(0)
    products(0, 0)
    products(0, 1)
    first_totals(0)
    first_stage(0)
    m1.relay(2)
    lax.fori_loop(0, 4, target_second, 0)
    second_totals(0)

    softmax(1)
    share(1, 10, 0, xn)
    share(1, 10, 3, yn)
    second_stage(0)
    sibling_rows(1)
    products(1, 0)
    products(1, 1)
    first_totals(1)
    relays(m2, 0)
    first_stage(1)
    m1.relay(6)
    relays(g2, 0)
    second_totals(1)
    m1.relay(7)
    main_last(0)
    second_stage(1)
    lax.fori_loop(0, 4, target_last, 0)
    g1.drain()
    m1.drain()
    relays(m2, 4)
    g2.drain()
    for copy in sends:
        copy.wait_send()

    for z in range(2):
        recv(st_in.at[z, 9], xs_s.at[0], xs_r.at[z, 3])
    st_in[zh, 14] = merge(st_in[zh, 13], st_in[zh, 9])
    whole = st_in[zh, 14, p_mine // 2]
    shift = whole[2:3] / whole[1:2]
    mean_logit = whole[3:4] / whole[1:2]
    lines = []
    for slot in (13, 9):
        lines += [line / whole[1:2] for line in factors(st_in[zh, slot, p_mine // 2], whole)]
    weight = 1.0 / whole[5:6]
    lines += [weight, mean_logit - whole[6:7] * weight, whole[4:5] / whole[1:2] - shift * mean_logit]
    columns_of(lines, fin3)

    main_last(1)

    rows = pl.ds(pl.multiple_of(x * 32 + zh * 16, 16), 16)
    norms = norm_col[zh, p_mine, pl.ds(pl.multiple_of(x * 16, 16), 16), :]
    inverse = norms[:, 0:1]
    columns = fin3[pl.ds(pl.multiple_of((p_mine % 2) * 64 + x * 16, 16), 16), :]

    def column(place):
        return columns[:, place : place + 1]

    def finish_chunk(n, carry):
        cols = pl.ds(pl.multiple_of(n * 512, 512), 512)
        far = pl.ds(pl.multiple_of(s * depth + n * 512, 512), 512)
        last_copy(gs3, gr3, gz_s, gz_r, n, n).wait_recv()
        last_copy(s3, r3, z_s, z_r, n, n).wait_recv()
        inputs = hid[p_mine, rows, cols].astype(F32) + steer[:, far]
        place = zh * 4 + n
        e_own, e_far = t2[place, 0], r3[n, 0].astype(F32)
        f_own, f_far = t2[place, 1], r3[n, 1].astype(F32)
        targets = gt2[n, 0, zh] + gr3[n, 0].astype(F32)
        grad = column(0) * e_own + column(2) * e_far - column(4) * targets
        ggn = column(0) * f_own + column(1) * e_own + column(2) * f_far + column(3) * e_far
        for o, back in enumerate((grad, ggn)):
            slope = column(5 + o) * inverse * (1.0 / full)
            out[o, :, cols] = gain[:, far] * back * inverse
            out_sub[o, :, cols] = inputs * slope * inverse
        return carry

    lax.fori_loop(0, 4, finish_chunk, 0)

    m2.drain()
    rc(st_in.at[:, 0:10], st_in.at[:, 0:10], xs_s.at[0], xs_r.at[0, 0], sib).wait_send()
    rc(code_out, code_out, cs_s.at[0], cs_r.at[0, 0], sib).wait_send()
    for n in range(4):
        last_copy(gs3, gr3, gz_s, gz_r, n, n).wait_send()
        last_copy(s3, r3, z_s, z_r, n, n).wait_send()


def body(hidden, steer, tangent, gain, head, target):
    vmem = pltpu.VMEM
    dma = pltpu.SemaphoreType.DMA
    any_spec = pl.BlockSpec(memory_space=pl.ANY)
    vmem_spec = pl.BlockSpec(memory_space=pltpu.VMEM)
    result, less = pl.pallas_call(
        kernel,
        out_shape=[jax.ShapeDtypeStruct((2, 16, 2048), F32)] * 2,
        in_specs=[any_spec] * 3 + [vmem_spec] * 3,
        out_specs=[vmem_spec] * 2,
        scratch_shapes=[
            vmem((128, 8192), BF16),
            vmem((4, 128, 2048), BF16),
            vmem((4, 8, 128), F32),
            vmem((128, 128), F32),
            vmem((2048, 2432), BF16),
            vmem((272, 2048), BF16),
            vmem((256, 2048), BF16),
            vmem((4, 1, 2432), F32),
            vmem((1, 2432), F32),
            vmem((2, 4, 64, 2432), F32),
            vmem((2, 4, 64, 2432), F32),
            vmem((2, 2, 64, 2432), BF16),
            vmem((2, 4, 64, 2432), BF16),
            vmem((4, 128, 2432), BF16),
            vmem((2, 2, 4, 64, 2432), BF16),
            vmem((2, 4, 64, 128), F32),
            vmem((2, 2, 128, 128), F32),
            vmem((2, 15, 2, 8, 128), F32),
            vmem((2, 128, 128), F32),
            vmem((4, 4, 64, 128), F32),
            vmem((2, 2, 128, 128), F32),
            vmem((128, 128), F32),
            vmem((2, 8, 2, 4, 2, 64, 128), BF16),
            vmem((2, 8, 2, 3, 2, 64, 128), BF16),
            vmem((2, 8, 2, 4, 2, 16, 128), BF16),
            vmem((2, 8, 2, 3, 2, 16, 128), BF16),
            vmem((8, 2, 16, 512), F32),
            vmem((8, 2, 16, 512), BF16),
            vmem((4, 2, 16, 512), BF16),
            vmem((2, 4, 2, 4, 1, 128, 128), BF16),
            vmem((2, 4, 2, 3, 1, 128, 128), BF16),
            vmem((2, 4, 2, 4, 1, 32, 128), BF16),
            vmem((2, 4, 2, 3, 1, 32, 128), BF16),
            vmem((4, 1, 2, 16, 512), F32),
            vmem((4, 1, 16, 512), BF16),
            vmem((4, 1, 16, 512), BF16),
            dma((4,)),
            dma((1,)), dma((4,)),
            dma((2, 2)), dma((2, 2)),
            dma((2, 2, 4)), dma((2, 2, 4)),
            dma((3,)), dma((4,)),
            dma((3,)), dma((4,)),
            dma((2,)), dma((4,)),
            dma((1,)), dma((2,)),
            dma((2, 5)), dma((2, 5)),
            dma((1,)), dma((2, 2)),
            dma((2, 3)), dma((2, 3)),
            dma((1,)), dma((2, 4)),
            dma((1,)), dma((8, 2)),
            dma((1,)), dma((8, 2)),
            dma((4,)), dma((4,)),
            dma((1,)), dma((4, 2)),
            dma((1,)), dma((4, 2)),
            dma((4,)), dma((4,)),
        ],
        compiler_params=pltpu.CompilerParams(
            collective_id=0, has_side_effects=True, vmem_limit_bytes=64 * 1024 * 1024 - 65536
        ),
    )(hidden, head, target, steer.reshape(1, -1), tangent.reshape(1, -1), gain.reshape(1, -1))
    return result[0] - less[0], result[1] - less[1]


def solution(mesh):
    return jax.shard_map(
        body,
        mesh=mesh,
        in_specs=(P("seq", None), P(), P(), P(), P("seq", "vocab"), P("seq", "vocab")),
        out_specs=(P("vocab", "seq"), P("vocab", "seq")),
        check_vma=False,
    )
```
